32 devices in a mesh: dp: 2 (over x), row: 4 (over y, core), col: 4 (over z).
Axes of the slice: x: 2, y: 2, z: 4, core: 2. Of those that a mesh axis runs over, the one named last changes fastest.
Arguments:
- acts: bfloat16 [1024, 8192], P(('dp', 'col'), 'row'), may hold values from -0.5 to 0.5
- grad_out: bfloat16 [1024, 14336], P(('dp', 'row'), 'col'), may hold values from -6 to 6
- weight: bfloat16 [8192, 14336], P('row', 'col'), may hold values from -0.0625 to 0.0625
Outputs:
- grad_input: bfloat16 [1024, 8192], P(('dp', 'col'), 'row')
- grad_weight: bfloat16 [4, 2048, 14336], P('row', 'dp', 'col')
The draws below stay inside these ranges and needn't reach their ends.
All inputs are finite; a program needn't handle non-finite values.
Results may differ from the reference program's by a relative error of at most 0.001.
Values may be sent and summed in bfloat16 or wider, within the bound.
No kernel may reach another device: no remote copies, remote signals or barrier semaphores. Data moves between devices by JAX's collectives and lax.ppermute only.
A program may use at most 128 MiB of HBM per device.

```python
import jax
import jax.numpy as jnp

D = 8192
FF = 14336
FRAMES = 1024
N_ROW = 4


def strengthened(values, rng, source, target, shards_of, factor):
    owner, partner = [(jnp.arange(values.shape[axis_at]) // (values.shape[axis_at] // shards_of)).reshape([-1 if axis == axis_at else 1 for axis in range(values.ndim)]) for axis_at in (source, target)]
    chosen = jax.random.permutation(rng, shards_of)[partner]
    strong = (owner == chosen) | (owner == (partner + shards_of // 2) % shards_of)
    return jnp.where(strong, factor * values, values)


def shard_levels(stream_key, shape, split, smallest, largest):
    def one(position, shards_of):
        heights = jax.random.uniform(jax.random.fold_in(jax.random.fold_in(stream_key, 6), position), (shards_of,), jnp.float32, smallest / len(split), largest / len(split))
        return jnp.repeat(jnp.exp(heights), shape[position] // shards_of).reshape((-1,) + (1,) * (len(shape) - position - 1))

    factor_of = one(*split[0])
    for cut in split[1:]:
        factor_of = factor_of * one(*cut)
    return factor_of


def centred(stream_key, shape, spread, bound, cuts=(), held_as=jnp.bfloat16):
    gain = shard_levels(stream_key, shape, cuts, -0.22, 0.18) if cuts else 1.0
    values = jax.random.normal(stream_key, shape, jnp.float32) * spread * gain
    return jnp.minimum(jnp.maximum(values, -bound), bound).astype(held_as)


def noise_with(own_key, shape, spread, most, pieces, heavy, kind=jnp.bfloat16):
    values = spread * jax.random.normal(own_key, shape, jnp.float32)
    if pieces:
        values = values * shard_levels(own_key, shape, pieces, -0.22, 0.18)
    return jnp.clip(strengthened(values, jax.random.fold_in(own_key, 3), *heavy), -most, most).astype(kind)


def setup_inputs(seed: int = 0) -> dict:
    arg_keys = jax.random.split(jax.random.key(seed), 4)
    acts = centred(arg_keys[0], (FRAMES, D), (FRAMES ** -0.5), 0.5, ((0, 8), (1, 4)))
    grad_out = noise_with(arg_keys[1], (FRAMES, FF), 1.0, 6.0, ((0, 8), (1, 4)), (0, 1, 8, 2.0))
    weight = centred(arg_keys[2], (D, FF), D ** -0.5, 0.0625, ((0, 4), (1, 4)))
    return dict(acts=acts, grad_out=grad_out, weight=weight)


def reference(acts, grad_out, weight):
    grad_input = jnp.dot(grad_out, weight.T, preferred_element_type=jnp.float32).astype(jnp.bfloat16)
    full = jnp.dot(acts.T, grad_out, preferred_element_type=jnp.float32)
    grad_weight = full.astype(jnp.bfloat16).reshape(N_ROW, D // N_ROW, FF)
    return grad_input, grad_weight
```

```python
import functools
import math

import jax
import jax.numpy as jnp
from jax import lax
from jax.experimental import pallas as pl
from jax.experimental.pallas import tpu as pltpu
from jax.sharding import PartitionSpec as P

AXES = ("dp", "row", "col")

MU = 16.0
OFFSET = 124.0
SLOPE = 2.0 * OFFSET / math.log2(1.0 + MU)
LANES = 128


def encode(z):
    top = jnp.maximum(jnp.max(jnp.abs(z), axis=1, keepdims=True) * 1.01, 1e-30)
    top = lax.reduce_precision(top, 8, 7)
    y = jnp.exp2(SLOPE * jnp.log2(1.0 + jnp.abs(z) * (MU / top)) - OFFSET)
    y = jnp.where(z < 0, -y, y)
    top = jnp.broadcast_to(top, (z.shape[0], LANES))
    return jnp.concatenate([y, top], axis=1).astype(jnp.bfloat16)


def decode(code):
    code = code.astype(jnp.float32)
    y, top = code[:, :-LANES], code[:, -LANES : 1 - LANES]
    t = jnp.exp2((jnp.log2(jnp.abs(y)) + OFFSET) * (1.0 / SLOPE)) - 1.0
    return jnp.where(y < 0, -t, t) * (top * (1.0 / MU))


def product(ga, gb, weight):
    g = jnp.concatenate([ga, gb], axis=0)
    return lax.dot_general(g, weight, (((1,), (1,)), ((), ())), preferred_element_type=jnp.float32)


def grad_kernel(n_blocks, tile, slot_ref, *refs):
    a_refs, g_refs = refs[:6], refs[6 : 6 + n_blocks]
    out_ref, a_vmem, at_ref, g_vmem, a_sem, g_sem = refs[6 + n_blocks :]
    rows = a_refs[0].shape[0]
    frames = rows // 2
    t = pl.program_id(0)

    def fetch(step, slot):
        cols = pl.ds(pl.multiple_of(step * tile, tile), tile)
        return [
            pltpu.make_async_copy(
                ref.at[pl.ds(b * frames, frames), cols],
                g_vmem.at[slot, pl.ds(i * frames, frames)],
                g_sem.at[slot, i],
            )
            for i, (ref, b) in enumerate(zip(g_refs, BLOCK_OF))
        ]

    def a_copy(i, k):
        return pltpu.make_async_copy(a_refs[k], a_vmem.at[i], a_sem.at[i])

    inner = slot_ref[4] != 0

    @pl.when(t == 0)
    def _():
        for i in (0, 1):
            a_copy(i, i).start()

        @pl.when(inner)
        def _():
            a_copy(2, 2).start()
            a_copy(3, 3).start()

        @pl.when(jnp.logical_not(inner))
        def _():
            a_copy(2, 4).start()
            a_copy(3, 5).start()

        for copy in fetch(0, 0):
            copy.start()
        for i in range(4):
            a_copy(i, i).wait()
            where = pl.ds(pl.multiple_of(slot_ref[i] * rows, rows), rows)
            at_ref[:, where] = a_vmem[i].T

    slot = lax.rem(t, 2)

    @pl.when(t + 1 < pl.num_programs(0))
    def _():
        for copy in fetch(t + 1, 1 - slot):
            copy.start()

    for copy in fetch(t, slot):
        copy.wait()
    full = jnp.dot(at_ref[...], g_vmem[slot], preferred_element_type=jnp.float32)
    out_ref[...] = full.astype(jnp.bfloat16)[None]


BLOCK_OF = (0, 0, 0, 0, 0, 0, 0, 1)


def grad(slots, a_blocks, g_parts):
    rows, width = a_blocks[0].shape
    depth = g_parts[0][0].shape[1]
    frames = rows // 2
    total = frames * len(g_parts)
    tile = 512
    return pl.pallas_call(
        functools.partial(grad_kernel, len(g_parts), tile),
        grid_spec=pltpu.PrefetchScalarGridSpec(
            num_scalar_prefetch=1,
            grid=(depth // tile,),
            in_specs=[pl.BlockSpec(memory_space=pl.ANY)] * (6 + len(g_parts)),
            out_specs=pl.BlockSpec((1, width, tile), lambda t, *_: (0, 0, t)),
            scratch_shapes=[
                pltpu.VMEM((4, rows, width), jnp.bfloat16),
                pltpu.VMEM((width, total), jnp.bfloat16),
                pltpu.VMEM((2, total, tile), jnp.bfloat16),
                pltpu.SemaphoreType.DMA((4,)),
                pltpu.SemaphoreType.DMA((2, len(g_parts))),
            ],
        ),
        out_shape=jax.ShapeDtypeStruct((1, width, depth), jnp.bfloat16),
        cost_estimate=pl.CostEstimate(
            flops=2 * total * width * depth,
            bytes_accessed=2 * (width + total) * depth,
            transcendentals=0,
        ),
        name="grad",
    )(slots, *a_blocks, *[g for g, _ in g_parts])


def fast(shape, acts, grad_out, weight):
    nd, nr, nc = (shape[a] for a in AXES)
    d, r, c = (lax.axis_index(a) for a in AXES)
    core = r % 2

    def exchange(x, to):
        pairs = []
        for i in range(nd):
            for j in range(nr):
                for k in range(nc):
                    there = to(i, j, k)
                    if there is not None:
                        m = (there[0] * nr + there[1]) * nc + there[2]
                        pairs.append(((i * nr + j) * nc + k, m))
        return lax.ppermute(x, AXES, pairs)

    over_x = lambda i, j, k: (1 - i, j, k)
    over_y = lambda i, j, k: (i, j ^ 2, k)
    over_core = lambda i, j, k: (i, j ^ 1, k)
    over_z = lambda i, j, k: (i, j, k ^ 1)
    middle = lambda i, j, k: (i, j, nc - 1 - k) if k in (1, 2) else None
    outward = lambda i, j, k: (i, j, k ^ 1) if k in (1, 2) else None
    early_z = lambda i, j, k: (i, j, k ^ 2) if k // 2 != j // 2 else None
    late_z = lambda i, j, k: (i, j, k ^ 2) if k // 2 == j // 2 else None

    frames, half = grad_out.shape[0], acts.shape[1] // 2
    scalars = lambda *v: jnp.stack([jnp.asarray(x, jnp.int32) for x in v])

    def pick(z, e):
        return lax.dynamic_slice_in_dim(z, frames * (e ^ core), frames, 0)

    keep, send = c % 2, 1 - c % 2
    g1 = exchange(grad_out, over_core)
    g2 = exchange(grad_out, over_y)
    other = lax.dynamic_slice_in_dim(acts, (1 - d) * half, half, 1)
    a_x = exchange(other, over_x)
    a0 = jnp.concatenate([lax.dynamic_slice_in_dim(acts, d * half, half, 1), a_x], axis=0)
    a_z = exchange(a0, over_z)
    a_m = exchange(a0, middle)
    z_e = product(grad_out, g1, weight)
    code = encode(pick(z_e, send))
    e_in = exchange(code, over_z)
    gx = exchange(grad_out, over_x)
    g3 = exchange(g2, over_core)
    a_m2 = exchange(a_z, middle)
    a_o = exchange(a_m, outward)
    z_l = product(g2, g3, weight)
    code = encode(pick(z_l, send))
    l_in = exchange(code, over_z)
    e_sum = pick(z_e, keep) + decode(e_in)
    code = encode(e_sum)
    e_last = exchange(code, early_z)
    a_o2 = exchange(a_m2, outward)
    gxy = exchange(gx, over_y)
    l_sum = pick(z_l, keep) + decode(l_in)
    code = encode(l_sum)
    l_last = exchange(code, late_z)
    gx2 = jnp.concatenate([gx, gxy], axis=0)
    gx4 = exchange(gx2, over_core)

    inner = ((c == 1) | (c == 2)).astype(jnp.int32)
    second = r ^ c ^ (2 + inner)
    slots = scalars(r ^ c, r ^ c ^ 1, second, second ^ 1, inner)
    grad_weight = grad(
        slots,
        [a0, a_z, a_m, a_m2, a_o, a_o2],
        [(grad_out, 0), (gx, 0), (g1, 0), (gx4, 0), (g2, 0), (gxy, 0), (g3, 0), (gx4, 1)],
    )
    early = r // 2 == c // 2
    grad_input = jnp.where(early, e_sum, l_sum) + decode(jnp.where(early, e_last, l_last))
    return grad_input.astype(jnp.bfloat16), grad_weight


def general(acts, grad_out, weight):
    act_local = lax.all_gather(acts, "col", axis=0, tiled=True)
    partial_value = lax.dot_general(
        lax.all_gather(grad_out, "row", axis=0, tiled=True),
        weight,
        (((1,), (1,)), ((), ())),
        preferred_element_type=jnp.float32,
    )
    act_all = lax.all_to_all(act_local, "dp", split_axis=1, concat_axis=0, tiled=True)
    summed = lax.dot_general(
        act_all,
        lax.all_gather(grad_out, ("dp", "row"), axis=0, tiled=True),
        (((0,), (0,)), ((), ())),
        preferred_element_type=jnp.float32,
    )
    grad_weight = summed.astype(jnp.bfloat16)[None]
    grad_input = lax.psum_scatter(partial_value, "col", scatter_dimension=0, tiled=True).astype(
        jnp.bfloat16
    )
    return (grad_input, grad_weight)


def solution(mesh):
    in_specs = (P(("dp", "col"), "row"), P(("dp", "row"), "col"), P("row", "col"))
    out_specs = (P(("dp", "col"), "row"), P("row", "dp", "col"))
    shape = dict(mesh.shape)
    specs = dict(mesh=mesh, in_specs=in_specs, out_specs=out_specs, check_vma=False)
    if (shape["dp"], shape["row"], shape["col"]) != (2, 4, 4):
        return jax.shard_map(general, **specs)

    def body(*args):
        return fast(shape, *args)

    return jax.shard_map(body, **specs)
```

```python
import functools
import math

import jax
import jax.numpy as jnp
from jax import lax
from jax.experimental import pallas as pl
from jax.experimental.pallas import tpu as pltpu
from jax.sharding import PartitionSpec as P

AXES = ("dp", "row", "col")

MU = 16.0
OFFSET = 124.0
SLOPE = 2.0 * OFFSET / math.log2(1.0 + MU)
SCALE_ROWS = 8


def encode(z):
    top = jnp.maximum(jnp.max(jnp.abs(z), axis=0, keepdims=True) * 1.01, 1e-30)
    top = lax.reduce_precision(top, 8, 7)
    y = jnp.exp2(SLOPE * jnp.log2(1.0 + jnp.abs(z) * (MU / top)) - OFFSET)
    y = jnp.where(z < 0, -y, y).astype(jnp.bfloat16)
    top = jnp.broadcast_to(top.astype(jnp.bfloat16), (SCALE_ROWS, z.shape[1]))
    return jnp.concatenate([y, top], axis=0)


def decode(code):
    y = code[:-SCALE_ROWS].astype(jnp.float32)
    top = code[-SCALE_ROWS : 1 - SCALE_ROWS].astype(jnp.float32)
    t = jnp.exp2((jnp.log2(jnp.abs(y)) + OFFSET) * (1.0 / SLOPE)) - 1.0
    return jnp.where(y < 0, -t, t) * (top * (1.0 / MU))


def product(ga, gb, weight):
    g = jnp.concatenate([ga, gb], axis=0)
    return lax.dot_general(g, weight, (((1,), (1,)), ((), ())), preferred_element_type=jnp.float32)


def grad_kernel(n_blocks, tile, slot_ref, *refs):
    a_refs, g_refs = refs[:6], refs[6 : 6 + n_blocks]
    out_ref, a_vmem, at_ref, g_vmem, a_sem, g_sem = refs[6 + n_blocks :]
    rows = a_refs[0].shape[0]
    frames = rows // 2
    t = pl.program_id(0)

    def fetch(step, slot):
        cols = pl.ds(pl.multiple_of(step * tile, tile), tile)
        return [
            pltpu.make_async_copy(
                ref.at[:, cols],
                g_vmem.at[slot, pl.ds(i * frames, frames)],
                g_sem.at[slot, i],
            )
            for i, ref in enumerate(g_refs)
        ]

    def a_copy(i, k):
        return pltpu.make_async_copy(a_refs[k], a_vmem.at[i], a_sem.at[i])

    inner = slot_ref[4] != 0

    @pl.when(t == 0)
    def _():
        for i in (0, 1):
            a_copy(i, i).start()

        @pl.when(inner)
        def _():
            a_copy(2, 2).start()
            a_copy(3, 3).start()

        @pl.when(jnp.logical_not(inner))
        def _():
            a_copy(2, 4).start()
            a_copy(3, 5).start()

        for copy in fetch(0, 0):
            copy.start()
        for i in range(4):
            a_copy(i, i).wait()
            where = pl.ds(pl.multiple_of(slot_ref[i] * rows, rows), rows)
            at_ref[:, where] = a_vmem[i].T

    slot = lax.rem(t, 2)

    @pl.when(t + 1 < pl.num_programs(0))
    def _():
        for copy in fetch(t + 1, 1 - slot):
            copy.start()

    for copy in fetch(t, slot):
        copy.wait()
    full = jnp.dot(at_ref[...], g_vmem[slot], preferred_element_type=jnp.float32)
    out_ref[...] = full.astype(jnp.bfloat16)[None]


def grad(slots, a_blocks, g_parts):
    rows, width = a_blocks[0].shape
    depth = g_parts[0].shape[1]
    frames = rows // 2
    total = frames * len(g_parts)
    tile = 512
    return pl.pallas_call(
        functools.partial(grad_kernel, len(g_parts), tile),
        grid_spec=pltpu.PrefetchScalarGridSpec(
            num_scalar_prefetch=1,
            grid=(depth // tile,),
            in_specs=[pl.BlockSpec(memory_space=pl.ANY)] * (6 + len(g_parts)),
            out_specs=pl.BlockSpec((1, width, tile), lambda t, *_: (0, 0, t)),
            scratch_shapes=[
                pltpu.VMEM((4, rows, width), jnp.bfloat16),
                pltpu.VMEM((width, total), jnp.bfloat16),
                pltpu.VMEM((2, total, tile), jnp.bfloat16),
                pltpu.SemaphoreType.DMA((4,)),
                pltpu.SemaphoreType.DMA((2, len(g_parts))),
            ],
        ),
        out_shape=jax.ShapeDtypeStruct((1, width, depth), jnp.bfloat16),
        cost_estimate=pl.CostEstimate(
            flops=2 * total * width * depth,
            bytes_accessed=2 * (width + total) * depth,
            transcendentals=0,
        ),
        name="grad",
    )(slots, *a_blocks, *g_parts)


def fast(shape, acts, grad_out, weight):
    nd, nr, nc = (shape[a] for a in AXES)
    d, r, c = (lax.axis_index(a) for a in AXES)
    core = r % 2

    def exchange(x, to):
        pairs = []
        for i in range(nd):
            for j in range(nr):
                for k in range(nc):
                    there = to(i, j, k)
                    if there is not None:
                        m = (there[0] * nr + there[1]) * nc + there[2]
                        pairs.append(((i * nr + j) * nc + k, m))
        return lax.ppermute(x, AXES, pairs)

    over_x = lambda i, j, k: (1 - i, j, k)
    over_y = lambda i, j, k: (i, j ^ 2, k)
    over_core = lambda i, j, k: (i, j ^ 1, k)
    over_z = lambda i, j, k: (i, j, k ^ 1)
    middle = lambda i, j, k: (i, j, nc - 1 - k) if k in (1, 2) else None
    outward = lambda i, j, k: (i, j, k ^ 1) if k in (1, 2) else None


    def line(j, k):
        return k if j // 2 else nc - 1 - k

    def along(*moves):
        to = dict(moves)

        def there(i, j, k):
            q = to.get(line(j, k))
            return None if q is None else (i, j, q if j // 2 else nc - 1 - q)

        return there

    late_z = lambda i, j, k: (i, j, k ^ 2) if k // 2 == j // 2 else None

    frames, half = grad_out.shape[0], acts.shape[1] // 2
    scalars = lambda *v: jnp.stack([jnp.asarray(x, jnp.int32) for x in v])

    def pick(z, e):
        return lax.dynamic_slice_in_dim(z, frames * (e ^ core), frames, 0)

    keep, send = c % 2, 1 - c % 2
    g1 = exchange(grad_out, over_core)
    g2 = exchange(grad_out, over_y)
    other = lax.dynamic_slice_in_dim(acts, (1 - d) * half, half, 1)
    a_x = exchange(other, over_x)
    a0 = jnp.concatenate([lax.dynamic_slice_in_dim(acts, d * half, half, 1), a_x], axis=0)
    a_z = exchange(a0, over_z)
    a_m = exchange(a0, middle)
    z_e = product(grad_out, g1, weight)
    q = jnp.where(r // 2 == 1, c, nc - 1 - c)
    far, near = r // 2, 1 - r // 2
    code = encode(pick(z_e, jnp.where(q == 0, far, near)))
    e_one = exchange(code, along((0, 1), (3, 2)))
    gx = exchange(grad_out, over_x)
    g3 = exchange(g2, over_core)
    a_m2 = exchange(a_z, middle)
    a_o = exchange(a_m, outward)
    z_l = product(g2, g3, weight)
    code = encode(pick(z_l, send))
    l_in = exchange(code, over_z)
    e_part = decode(e_one)
    code = encode(pick(z_e, jnp.where(q == 0, near, far)) + e_part)
    e_sum = lax.optimization_barrier(pick(z_e, jnp.where(q == 3, far, near)) + e_part)
    e_two = exchange(code, along((0, 1), (1, 2)))
    a_o2 = exchange(a_m2, outward)
    gxy = exchange(gx, over_y)
    gx1 = exchange(gx, over_core)
    l_sum = pick(z_l, keep) + decode(l_in)
    code = encode(l_sum)
    l_sum = lax.optimization_barrier(l_sum)
    l_last = exchange(code, late_z)
    base = lax.optimization_barrier(jnp.where(r // 2 == c // 2, e_sum, l_sum))
    code = encode(pick(z_e, jnp.where(q == 1, near, far)) + decode(e_two))
    e_three = exchange(code, along((1, 2), (2, 3)))
    gx3 = exchange(gxy, over_core)

    inner = ((c == 1) | (c == 2)).astype(jnp.int32)
    second = r ^ c ^ (2 + inner)
    slots = scalars(r ^ c, r ^ c ^ 1, second, second ^ 1, inner)
    grad_weight = grad(
        slots,
        [a0, a_z, a_m, a_m2, a_o, a_o2],
        [grad_out, gx, g1, gx1, g2, gxy, g3, gx3],
    )
    grad_input = base + decode(e_three.astype(jnp.float32) + l_last.astype(jnp.float32))
    return grad_input.astype(jnp.bfloat16), grad_weight


def general(acts, grad_out, weight):
    act_local = lax.all_gather(acts, "col", axis=0, tiled=True)
    partial_value = lax.dot_general(
        lax.all_gather(grad_out, "row", axis=0, tiled=True),
        weight,
        (((1,), (1,)), ((), ())),
        preferred_element_type=jnp.float32,
    )
    act_all = lax.all_to_all(act_local, "dp", split_axis=1, concat_axis=0, tiled=True)
    summed = lax.dot_general(
        act_all,
        lax.all_gather(grad_out, ("dp", "row"), axis=0, tiled=True),
        (((0,), (0,)), ((), ())),
        preferred_element_type=jnp.float32,
    )
    grad_weight = summed.astype(jnp.bfloat16)[None]
    grad_input = lax.psum_scatter(partial_value, "col", scatter_dimension=0, tiled=True).astype(
        jnp.bfloat16
    )
    return (grad_input, grad_weight)


def solution(mesh):
    in_specs = (P(("dp", "col"), "row"), P(("dp", "row"), "col"), P("row", "col"))
    out_specs = (P(("dp", "col"), "row"), P("row", "dp", "col"))
    shape = dict(mesh.shape)
    specs = dict(mesh=mesh, in_specs=in_specs, out_specs=out_specs, check_vma=False)
    if (shape["dp"], shape["row"], shape["col"]) != (2, 4, 4):
        return jax.shard_map(general, **specs)

    def body(*args):
        return fast(shape, *args)

    return jax.shard_map(body, **specs)
```
